32 devices in a mesh: frame: 2 (over y), orient: 4 (over x, core), pix: 4 (over z).
Axes of the slice: x: 2, y: 2, z: 4, core: 2. Of those that a mesh axis runs over, the one named last changes fastest.
Arguments:
- photon_counts: int32 [32, 16384], P('frame', 'pix'), may hold values from 0 to 8, as said below
- slices: bfloat16 [768, 16384], P('orient', 'pix'), may hold values from 0.049804688 to 2
- owner_ids: int32 [768, 128], P('orient', 'pix'), may hold values from 0 to 3
- tile_ids: int32 [768, 128], P('orient', 'pix'), may hold values from 0 to 2047
- patch_count: int32 [768], P('orient'), may hold values from 16 to 128
- old_model: float32 [1024, 128], P(('frame', 'orient', 'pix')), may hold values from 0.1 to 2
Outputs:
- orient_prob: bfloat16 [32, 768], P('frame', 'orient')
- merged: float32 [1024, 128], P(('frame', 'orient', 'pix'))
The draws below stay inside these ranges and needn't reach their ends.
Inputs may be any that keep to these rules, and one draw needn't show every extreme that they name: `photon_counts`: each frame's counts stay below a level of 3 to 9 drawn for that frame.
All inputs are finite; a program needn't handle non-finite values.
Results may differ from the reference program's by a relative error of at most 0.0029.
The reference program's roundings to bfloat16 on the way (of `log_slice` and `frames_bf`) count: a program that leaves them out, or rounds other values in their place, can miss the bound.
Values sent between devices are 32-bit elements; how exact they have to be, the bound alone decides.
No kernel may reach another device: no remote copies, remote signals or barrier semaphores. Data moves between devices by JAX's collectives and lax.ppermute only.
A program may use at most 64 MiB of HBM per device.

```python
import math
import jax
import jax.numpy as jnp
from jax import lax

P_SIZE = 16384
R = 768
NB = 4
BRICK_ROWS = 256
SHIFTS = 8
FRAMES = 32
NQ = 128
MROWS = 1024


def draw_photon_counts(key, part):
    first_key, second_key = jax.random.split(jax.random.fold_in(key, 11))
    level = jax.random.randint(first_key, (FRAMES, 1), 3, 10)
    return jax.random.randint(second_key, (FRAMES, P_SIZE), 0, level).astype(jnp.int32)


def touch_ends(entries, stream_key, low, top_value):
    spot = [jax.random.randint(jax.random.fold_in(stream_key, axis), (), 0, length) for axis, length in enumerate(entries.shape)]
    widest = entries.shape.index(max(entries.shape))
    neighbour = spot[:widest] + [(spot[widest] + 1) % entries.shape[widest]] + spot[widest + 1:]
    return entries.at[tuple(spot)].set(low).at[tuple(neighbour)].set(top_value)


def level_of(key, dims, cuts, least, largest):
    loudness = 1.0
    for axis_at, parts in cuts:
        draws = jax.random.uniform(jax.random.fold_in(jax.random.fold_in(key, 6), axis_at), (parts,), jnp.float32, least / len(cuts), largest / len(cuts))
        loudness = loudness * jnp.repeat(jnp.exp(draws), dims[axis_at] // parts).reshape((-1,) + (1,) * (len(dims) - 1 - axis_at))
    return loudness


def setup_inputs(seed: int = 0) -> dict:
    seeds = jax.random.split(jax.random.key(seed), 7)
    return {
        "photon_counts": draw_photon_counts(jax.random.fold_in(seeds[6], 71), 0),
        "slices": jnp.clip(jnp.exp(math.log(2.0) - 3.6927934 * jax.random.uniform(seeds[1], (R, P_SIZE), jnp.float32) ** level_of(seeds[1], (R, P_SIZE), ((0, 4), (1, 4)), -0.2, 0.2)), 0.049804688, 2.0).astype(jnp.bfloat16),
        "owner_ids": touch_ends(jax.random.randint(seeds[2], (R, NQ), 0, NB), jax.random.fold_in(seeds[2], 1), 0, NB - 1).astype(jnp.int32),
        "tile_ids": touch_ends(jax.random.randint(seeds[3], (R, NQ), 0, BRICK_ROWS * SHIFTS), jax.random.fold_in(seeds[3], 1), 0, (BRICK_ROWS * SHIFTS) - 1).astype(jnp.int32),
        "patch_count": touch_ends(jax.random.randint(seeds[4], (R,), NQ // 8, NQ + 1), jax.random.fold_in(seeds[4], 1), NQ // 8, NQ).astype(jnp.int32),
        "old_model": jnp.clip(jnp.exp(math.log(2.0) - 2.9957323 * jax.random.uniform(seeds[5], (MROWS, 128), jnp.float32) ** level_of(seeds[5], (MROWS, 128), ((0, 32),), -0.2, 0.2)), 0.1, 2.0),
    }


def deposit(values, weights, owners, tile_ids, live_mask, rows_total):
    shift_ids = tile_ids % SHIFTS
    row_index = owners * BRICK_ROWS + tile_ids // SHIFTS
    lanes = lax.iota(jnp.int32, 128)
    lane_index = (lanes[None, None, :] - 17 * shift_ids[:, :, None]) % 128
    moved = jnp.take_along_axis(values, lane_index, axis=2) * live_mask[:, :, None]
    flat_rows = row_index.reshape(-1)
    brick_sum = jnp.zeros((rows_total, 128), jnp.float32).at[flat_rows].add(moved.reshape(-1, 128))
    brick_weight = jnp.zeros((rows_total,), jnp.float32).at[flat_rows].add((live_mask * weights[:, None]).reshape(-1))
    return (brick_sum, brick_weight)

def reference(photon_counts, slices, owner_ids, tile_ids, patch_count, old_model):
    frames_bf = photon_counts.astype(jnp.bfloat16)
    log_slice = jnp.log(slices.astype(jnp.float32)).astype(jnp.bfloat16)
    fit = jnp.dot(frames_bf, log_slice.T, preferred_element_type=jnp.float32)
    slice_mass = lax.optimization_barrier(jnp.sum(slices.astype(jnp.float32), axis=1))
    score = (fit - slice_mass[None, :]) * (1.0 / math.sqrt(P_SIZE))
    score_top = lax.optimization_barrier(jnp.max(score, axis=1))
    weights_exp = jnp.exp(score - score_top[:, None])
    score_total = lax.optimization_barrier(jnp.sum(weights_exp, axis=1))
    orient_prob = (weights_exp / score_total[:, None]).astype(jnp.bfloat16)
    total_weight = lax.optimization_barrier(jnp.sum(orient_prob.astype(jnp.float32), axis=0))
    photon_sum = jnp.dot(orient_prob.T, frames_bf, preferred_element_type=jnp.float32)
    patch_id = lax.iota(jnp.int32, NQ)
    live_mask = (patch_id[None, :] < patch_count[:, None]).astype(jnp.float32)
    brick_sum, brick_weight = deposit(photon_sum.reshape(R, NQ, 128), total_weight, owner_ids, tile_ids, live_mask, MROWS)
    prior = FRAMES * NQ / (4.0 * MROWS)
    merged = (brick_sum + prior * old_model) / (brick_weight[:, None] + prior)
    return (orient_prob, merged)
```

```python
import functools
import math

import jax
import jax.numpy as jnp
from jax import lax
from jax.experimental import pallas as pl
from jax.experimental.pallas import tpu as pltpu
from jax.sharding import PartitionSpec as P

P_SIZE = 16384
NB = 4
BRICK_ROWS = 256
SHIFTS = 8
STEP = 17
LANES = 128


def joined(part, axis, combine):
    gathered = jax.tree.map(lambda a: lax.all_gather(a, axis), part)

    def take(source):
        return jax.tree.map(lambda a: lax.dynamic_index_in_dim(a, source, 0, False), gathered)

    return lax.fori_loop(
        1, lax.axis_size(axis), lambda source, state: combine(state, take(source)), take(0)
    )


def deposit(values, weights, owners, tile_ids, live_mask, rows_total):
    shift_ids = tile_ids % SHIFTS
    inner_rows = tile_ids // SHIFTS
    moved = jnp.zeros(values.shape, jnp.float32)
    for shift in range(SHIFTS):
        rolled = jnp.roll(values, STEP * shift, axis=2)
        moved = jnp.where((shift_ids == shift)[:, :, None], rolled, moved)
    flat_values = (moved * live_mask[:, :, None]).reshape(-1, LANES)
    flat_weights = (live_mask * weights[:, None]).reshape(-1, 1)
    flat_owners = owners.reshape(-1)
    flat_inner = inner_rows.reshape(-1)
    brick_lines = lax.iota(jnp.int32, BRICK_ROWS)

    def one_brick(brick):
        picked = (flat_inner[None, :] == brick_lines[:, None]) & (flat_owners[None, :] == brick)
        onehot = picked.astype(jnp.float32)
        summed = jnp.dot(
            onehot, flat_values, precision=lax.Precision.HIGHEST, preferred_element_type=jnp.float32
        )
        weighed = jnp.dot(
            onehot,
            flat_weights,
            precision=lax.Precision.HIGHEST,
            preferred_element_type=jnp.float32,
        )
        return (summed, weighed[:, 0])

    brick_sum, brick_weight = lax.map(one_brick, lax.iota(jnp.int32, rows_total // BRICK_ROWS))
    return (brick_sum.reshape(rows_total, LANES), brick_weight.reshape(rows_total))


def combine_stats(earlier, latter):
    score_top = jnp.maximum(earlier[0], latter[0])
    summed = earlier[1] * jnp.exp(earlier[0] - score_top) + latter[1] * jnp.exp(
        latter[0] - score_top
    )
    return (score_top, summed)


def general_shards(photon_counts, slices, owner_ids, tile_ids, patch_count, old_model):
    orient_rows = slices.shape[0]
    pixel_cols = slices.shape[1]
    local_patches = pixel_cols // LANES
    rows_total = NB * BRICK_ROWS
    frames_bf = photon_counts.astype(jnp.bfloat16)
    log_slice = jnp.log(slices.astype(jnp.float32)).astype(jnp.bfloat16)
    fit_part = jnp.einsum("fp,rp->fr", frames_bf, log_slice, preferred_element_type=jnp.float32)
    mass_part = jnp.sum(slices, axis=1, dtype=jnp.float32)
    fit, slice_mass = lax.psum((fit_part, mass_part), "pix")
    score = (fit - slice_mass[None, :]) * (1.0 / math.sqrt(P_SIZE))
    local_top = jnp.max(score, axis=1)
    local_total = jnp.sum(jnp.exp(score - local_top[:, None]), axis=1)
    score_top, score_total = joined((local_top, local_total), "orient", combine_stats)
    weights_exp = jnp.exp(score - score_top[:, None])
    orient_prob = (weights_exp / score_total[:, None]).astype(jnp.bfloat16)
    weight_part = jnp.sum(orient_prob.astype(jnp.float32), axis=0)
    photon_part = jnp.einsum(
        "fr,fp->rp", orient_prob, frames_bf, preferred_element_type=jnp.float32
    )
    pix_start = lax.axis_index("pix") * local_patches
    frame_count = lax.axis_size("frame")
    weight_tile = jnp.broadcast_to(weight_part[:, None], (orient_rows, frame_count))
    photon_sum, weight_sum = (
        lax.psum_scatter(photon_part, "frame", scatter_dimension=1, tiled=True),
        lax.psum_scatter(weight_tile, "frame", scatter_dimension=1, tiled=True),
    )
    held_patches = photon_sum.shape[1] // LANES
    frame_start = lax.axis_index("frame") * held_patches
    owner_part = lax.dynamic_slice_in_dim(owner_ids, frame_start, held_patches, 1)
    tile_part = lax.dynamic_slice_in_dim(tile_ids, frame_start, held_patches, 1)
    patch_id = pix_start + frame_start + lax.iota(jnp.int32, held_patches)
    live_mask = (patch_id[None, :] < patch_count[:, None]).astype(jnp.float32)
    brick_part, weight_rows = deposit(
        photon_sum.reshape(orient_rows, held_patches, LANES),
        weight_sum[:, 0],
        owner_part,
        tile_part,
        live_mask,
        rows_total,
    )
    brick_sum, brick_weight = (
        lax.psum_scatter(brick_part, ("frame", "orient", "pix"), scatter_dimension=0, tiled=True),
        lax.psum_scatter(weight_rows, ("frame", "orient", "pix"), scatter_dimension=0, tiled=True),
    )
    prior = prior_of(photon_counts, slices, rows_total)
    merged = (brick_sum + prior * old_model) / (brick_weight[:, None] + prior)
    return (orient_prob, merged)


def prior_of(photon_counts, slices, rows_total):
    frames_total = photon_counts.shape[0] * lax.axis_size("frame")
    patches_total = slices.shape[1] * lax.axis_size("pix") // LANES
    return frames_total * patches_total / (4.0 * rows_total)


def across(value, axis, mask):
    count = lax.axis_size(axis)
    return lax.ppermute(value, axis, [(i, i ^ mask) for i in range(count)])


def across_two(value, axes, masks):
    first, second = (lax.axis_size(axis) for axis in axes)
    pairs = [
        (i * second + j, (i ^ masks[0]) * second + (j ^ masks[1]))
        for i in range(first)
        for j in range(second)
    ]
    return lax.ppermute(value, axes, pairs)


def fit_kernel(counts_ref, slices_ref, out_ref, mass_acc, fit_acc):
    step = pl.program_id(0)

    @pl.when(step == 0)
    def _():
        mass_acc[...] = jnp.zeros_like(mass_acc)
        fit_acc[...] = jnp.zeros_like(fit_acc)

    wide = slices_ref[...].astype(jnp.float32)
    total = wide[:, :LANES]
    for start in range(LANES, wide.shape[1], LANES):
        total = total + wide[:, start : start + LANES]
    mass_acc[...] += total
    log_slice = jnp.log(wide).astype(jnp.bfloat16)
    frames_bf = counts_ref[...].astype(jnp.float32).astype(jnp.bfloat16)
    fit_acc[...] += lax.dot_general(
        frames_bf, log_slice, (((1,), (1,)), ((), ())), preferred_element_type=jnp.float32
    )

    @pl.when(step == pl.num_programs(0) - 1)
    def _():
        ones = jnp.ones((out_ref.shape[0], LANES), jnp.float32)
        mass = lax.dot_general(
            ones,
            mass_acc[...],
            (((1,), (1,)), ((), ())),
            precision=lax.Precision.HIGHEST,
            preferred_element_type=jnp.float32,
        )
        out_ref[...] = fit_acc[...] - mass


def fit_less_mass(photon_counts, slices):
    frames, pixels = photon_counts.shape
    orients = slices.shape[0]
    chunk = math.gcd(pixels, 1024)
    return pl.pallas_call(
        fit_kernel,
        grid=(pixels // chunk,),
        in_specs=[
            pl.BlockSpec((frames, chunk), lambda i: (0, i)),
            pl.BlockSpec((orients, chunk), lambda i: (0, i)),
        ],
        out_specs=pl.BlockSpec((frames, orients), lambda i: (0, 0)),
        out_shape=jax.ShapeDtypeStruct((frames, orients), jnp.float32),
        scratch_shapes=[
            pltpu.VMEM((orients, LANES), jnp.float32),
            pltpu.VMEM((frames, orients), jnp.float32),
        ],
        name="fit",
    )(photon_counts, slices)


def rolled_kernel(groups, *refs):
    count_refs, out_ref = refs[:-1], refs[-1]
    rows = count_refs[0].shape[0]
    for group, count_ref in enumerate(count_refs):
        for patch in range(out_ref.shape[0]):
            part = count_ref[:, patch * LANES : (patch + 1) * LANES].astype(jnp.float32)
            for shift in range(SHIFTS):
                turned = pltpu.roll(part, (STEP * shift) % LANES, 1) if shift else part
                at = (shift * groups + group) * rows
                out_ref[patch, at : at + rows, :] = turned.astype(jnp.bfloat16)


def rolled_frames(counts):
    frames, pixels = counts[0].shape
    patches = pixels // LANES
    block = math.gcd(patches, 4)
    return pl.pallas_call(
        functools.partial(rolled_kernel, len(counts)),
        grid=(patches // block,),
        in_specs=[pl.BlockSpec((frames, block * LANES), lambda i: (0, i)) for _ in counts],
        out_specs=pl.BlockSpec((block, SHIFTS * len(counts) * frames, LANES), lambda i: (i, 0, 0)),
        out_shape=jax.ShapeDtypeStruct(
            (patches, SHIFTS * len(counts) * frames, LANES), jnp.bfloat16
        ),
        name="rolled",
    )(*counts)


def deposit_kernel(groups, orients, scale, where_ref, *refs):
    score_refs = refs[: groups * orients]
    id_refs = refs[groups * orients : groups * orients + orients]
    rolled_ref = refs[groups * orients + orients]
    prob_ref = refs[groups * orients + orients + 1]
    piece_refs = refs[groups * orients + orients + 2 : -4]
    ids, probs, summed, weighed = refs[-4:]
    frames, width = score_refs[0].shape
    patches = rolled_ref.shape[0]
    rows = summed.shape[0]
    columns = orients * width

    for group in range(groups):
        scores = [score_refs[group * orients + b][...] * scale for b in range(orients)]
        top = functools.reduce(jnp.maximum, [jnp.max(s, axis=1, keepdims=True) for s in scores])
        parts = [jnp.exp(s - top) for s in scores]
        total = functools.reduce(jnp.add, [jnp.sum(s, axis=1, keepdims=True) for s in parts])
        for b in range(orients):
            prob = (parts[b] / total).astype(jnp.bfloat16)
            if group == 0 and b == 0:
                prob_ref[...] = prob
            probs[group * frames : (group + 1) * frames, b * width : (b + 1) * width] = prob.astype(
                jnp.float32
            )
    for b in range(orients):
        ids[:, b * width : (b + 1) * width] = id_refs[b][...]

    base = where_ref[0]
    lines = lax.broadcasted_iota(jnp.int32, (rows, columns), 0) + base
    summed[...] = jnp.zeros_like(summed)
    weighed[...] = jnp.zeros_like(weighed)

    def one_patch(patch, carry):
        row = ids[pl.ds(patch, 1), :]
        shift_of = ids[pl.ds(patches + patch, 1), :]
        onehot = jnp.where(row == lines, 1.0, 0.0).astype(jnp.bfloat16)
        prob = probs[...]
        masked = jnp.concatenate(
            [
                jnp.where(shift_of == shift, prob, 0.0).astype(jnp.bfloat16)
                for shift in range(SHIFTS)
            ],
            axis=0,
        )
        picked = lax.dot_general(
            onehot, masked, (((1,), (1,)), ((), ())), preferred_element_type=jnp.float32
        )
        weighed[...] += picked
        summed[...] += jnp.dot(
            picked.astype(jnp.bfloat16), rolled_ref[patch], preferred_element_type=jnp.float32
        )
        return carry

    lax.fori_loop(0, patches, one_patch, 0)

    heavy = jnp.broadcast_to(jnp.sum(weighed[...], axis=1, keepdims=True), (rows, LANES))
    weighed[:, :LANES] = heavy
    held = piece_refs[0].shape[0] // 2
    for k, piece in enumerate(piece_refs):
        start = pl.multiple_of((where_ref[1] ^ k) * held, held)
        piece[:held, :] = summed[pl.ds(start, held), :]
        piece[held:, :] = weighed[pl.ds(start, held), :LANES]


def deposited(where, scores, ids, rolled, groups, scale, rows, pieces):
    frames, width = scores[0].shape
    orients = len(ids)
    held = rows // pieces
    in_vmem = pl.BlockSpec(memory_space=pltpu.VMEM)
    columns = orients * width
    return pl.pallas_call(
        functools.partial(deposit_kernel, groups, orients, scale),
        in_specs=[pl.BlockSpec(memory_space=pltpu.SMEM)]
        + [in_vmem] * (len(scores) + len(ids) + 1),
        out_specs=[in_vmem] * (1 + pieces),
        out_shape=[jax.ShapeDtypeStruct((frames, width), jnp.bfloat16)]
        + [jax.ShapeDtypeStruct((2 * held, LANES), jnp.float32)] * pieces,
        scratch_shapes=[
            pltpu.VMEM((ids[0].shape[0], columns), jnp.int32),
            pltpu.VMEM((groups * frames, columns), jnp.float32),
            pltpu.VMEM((rows, LANES), jnp.float32),
            pltpu.VMEM((rows, rolled.shape[1]), jnp.float32),
        ],
        name="deposit",
    )(where, *scores, *ids, rolled)


def direct_shards(photon_counts, slices, owner_ids, tile_ids, patch_count, old_model):
    rows_total = NB * BRICK_ROWS
    local_patches = slices.shape[1] // LANES
    groups, orients, pieces = (lax.axis_size(axis) for axis in ("frame", "orient", "pix"))
    rows = rows_total // (groups * orients)
    pix_at = lax.axis_index("pix")

    counts = [photon_counts] + [across(photon_counts, "frame", g) for g in range(1, groups)]
    patch_id = pix_at * local_patches + lax.iota(jnp.int32, local_patches)
    row_index = owner_ids * BRICK_ROWS + tile_ids // SHIFTS
    row_index = jnp.where(patch_id[None, :] < patch_count[:, None], row_index, -1)
    own_ids = jnp.concatenate([row_index.T, (tile_ids % SHIFTS).T], axis=0)
    ids = [own_ids] + [across(own_ids, "orient", b) for b in range(1, orients)]
    rolled = rolled_frames(counts)

    part = fit_less_mass(photon_counts, slices)
    score = part + functools.reduce(jnp.add, [across(part, "pix", k) for k in range(1, pieces)])
    scores = [
        score if not (g or b) else across_two(score, ("frame", "orient"), (g, b))
        for g in range(groups)
        for b in range(orients)
    ]
    base = (lax.axis_index("frame") * orients + lax.axis_index("orient")) * rows
    where = jnp.stack([base, pix_at]).astype(jnp.int32)
    orient_prob, *own = deposited(
        where, scores, ids, rolled, groups, 1.0 / math.sqrt(P_SIZE), rows, pieces
    )
    total = own[0] + functools.reduce(jnp.add, [across(own[k], "pix", k) for k in range(1, pieces)])
    held = rows // pieces
    prior = prior_of(photon_counts, slices, rows_total)
    merged = (total[:held] + prior * old_model) / (total[held:] + prior)
    return (orient_prob, merged)


def solution(mesh):
    placed = (
        P("frame", "pix"),
        P("orient", "pix"),
        P("orient", "pix"),
        P("orient", "pix"),
        P("orient"),
        P(("frame", "orient", "pix"), None),
    )
    small = mesh.shape["frame"] <= 2 and all(
        mesh.shape[axis] in (1, 2, 4) for axis in ("orient", "pix")
    )
    return jax.shard_map(
        direct_shards if small else general_shards,
        mesh=mesh,
        in_specs=placed,
        out_specs=(P("frame", "orient"), P(("frame", "orient", "pix"), None)),
        check_vma=False,
    )
```
